512 devices in a mesh: energy: 32 (over y, x), chain: 16 (over z, core).
Axes of the slice: x: 4, y: 8, z: 8, core: 2. Of those that a mesh axis runs over, the one named last changes fastest.
Arguments:
- onsite: float32 [16, 2, 128, 128], P('chain'), may hold values from -0.5 to 0.5
- coupling: float32 [16, 2, 128, 128], P('chain'), may hold values from -0.3125 to 0.3125
- retained: int32 [16, 8192], P('chain'), may hold values from 0 to 16383
Outputs:
- polarization: float32 [2, 32, 16, 8192], P(None, None, 'chain', 'energy')
The draws below stay inside these ranges and needn't reach their ends.
All inputs are finite; a program needn't handle non-finite values.
Results may differ from the reference program's by a relative error of at most 0.0003.
Values sent between devices are 32-bit elements; how exact they have to be, the bound alone decides.
No kernel may reach another device: no remote copies, remote signals or barrier semaphores. Data moves between devices by JAX's collectives and lax.ppermute only.
A program may use at most 64 MiB of HBM per device.

```python
import math
import jax
import jax.numpy as jnp
from jax import lax

ORB = 128
NK = 8192
NE = 32
NB = 16


def touch_ends(result, rng, smallest, high):
    place = [jax.random.randint(jax.random.fold_in(rng, axis), (), 0, length) for axis, length in enumerate(result.shape)]
    widest = result.shape.index(max(result.shape))
    beside = place[:widest] + [(place[widest] + 1) % result.shape[widest]] + place[widest + 1:]
    return result.at[tuple(place)].set(smallest).at[tuple(beside)].set(high)


def shard_levels(own_key, dims, shards, smallest, largest):
    def one(dim, shards_of):
        draws = jax.random.uniform(jax.random.fold_in(jax.random.fold_in(own_key, 6), dim), (shards_of,), jnp.float32, smallest / len(shards), largest / len(shards))
        return jnp.repeat(jnp.exp(draws), dims[dim] // shards_of).reshape((-1,) + (1,) * (len(dims) - dim - 1))

    gain = one(*shards[0])
    for cut in shards[1:]:
        gain = gain * one(*cut)
    return gain


def centred(key, dims, scale, limit, split=(), held_as=jnp.bfloat16):
    array = jax.random.normal(key, dims, jnp.float32) * scale
    if len(split) > 0:
        array = shard_levels(key, dims, split, -0.22, 0.18) * array
    return jnp.clip(array, min=-limit, max=limit).astype(held_as)


def setup_inputs(seed: int = 0) -> dict:
    arg_keys = jax.random.split(jax.random.key(seed), 4)
    onsite = centred(arg_keys[0], (NB, 2, ORB, ORB), ORB ** -0.5, 0.5, ((0, 16),), jnp.float32)
    coupling = centred(arg_keys[1], (NB, 2, ORB, ORB), (3 * ORB) ** -0.5, 0.3125, ((0, 16),), jnp.float32)
    retained = touch_ends(jax.random.randint(arg_keys[2], (NB, NK), 0, ORB * ORB), jax.random.fold_in(arg_keys[2], 1), 0, (ORB * ORB) - 1).astype(jnp.int32)
    return {"onsite": onsite, "coupling": coupling, "retained": retained}


broadening = 0.04

def product(left_part, right_part):
    return jnp.matmul(left_part, right_part, precision=lax.Precision.HIGHEST)

def represent(real_part, imag_part):
    upper_half = jnp.concatenate([real_part, -imag_part], axis=-1)
    lower_half = jnp.concatenate([imag_part, real_part], axis=-1)
    return jnp.concatenate([upper_half, lower_half], axis=-2)

def hermitian(raw_block):
    real_part = 0.5 * (raw_block[0] + raw_block[0].T)
    imag_part = 0.5 * (raw_block[1] - raw_block[1].T)
    return represent(real_part, imag_part)

def contact_term(coupler):
    orbitals = coupler.shape[0] // 2
    square = product(coupler, coupler.T)
    return represent(0.5 * square[orbitals:, :orbitals], -0.5 * square[:orbitals, :orbitals])

def dft_tables(length):
    positions = jnp.arange(length, dtype=jnp.int32)
    phases = positions[:, None] * positions[None, :] % length
    angles = phases.astype(jnp.float32) * (2.0 * math.pi / length)
    return (jnp.cos(angles), jnp.sin(angles))

def correlate(left_real, left_imag, right_real, right_imag):
    cosine_table, sine_table = dft_tables(left_real.shape[0])
    turn_real = product(cosine_table, left_real) - product(sine_table, left_imag)
    turn_imag = product(cosine_table, left_imag) + product(sine_table, left_real)
    back_real = product(cosine_table, right_real) + product(sine_table, right_imag)
    back_imag = product(cosine_table, right_imag) - product(sine_table, right_real)
    prod_real = turn_real * back_real - turn_imag * back_imag
    prod_imag = turn_real * back_imag + turn_imag * back_real
    inverse_count = 1.0 / left_real.shape[0]
    out_real = (product(cosine_table, prod_real) - product(sine_table, prod_imag)) * inverse_count
    out_imag = (product(cosine_table, prod_imag) + product(sine_table, prod_real)) * inverse_count
    return (out_real, out_imag)

def pick_pairs(full_block, chosen, orbitals):
    energy_count = full_block.shape[0]
    real_flat = full_block[:, :orbitals, :orbitals].reshape(energy_count, orbitals * orbitals)
    imag_flat = full_block[:, orbitals:, :orbitals].reshape(energy_count, orbitals * orbitals)
    mirror = chosen % orbitals * orbitals + chosen // orbitals
    return (real_flat[:, chosen], imag_flat[:, chosen], real_flat[:, mirror], imag_flat[:, mirror])

def shifted_energy(energy, identity):
    return represent(energy * identity, broadening * identity)

def reference(onsite, coupling, retained):
    orbitals = onsite.shape[-1]
    energy_count = NE
    blocks = NB
    energies = -2.0 + 4.0 * jnp.arange(energy_count, dtype=jnp.float32) / energy_count
    identity = jnp.eye(orbitals, dtype=jnp.float32)
    shifted = jax.vmap(shifted_energy, in_axes=(0, None))(energies, identity)
    unit_wide = jnp.broadcast_to(jnp.eye(2 * orbitals, dtype=jnp.float32), shifted.shape)
    sigma_block = jnp.zeros_like(shifted)
    greens = []
    for block_index in range(blocks):
        coupler = represent(coupling[block_index, 0], coupling[block_index, 1])
        matrix = shifted - hermitian(onsite[block_index]) - sigma_block
        if block_index == blocks - 1:
            matrix = matrix - contact_term(coupler)
        inverse = jnp.linalg.solve(matrix, unit_wide)
        greens.append(inverse)
        sigma_block = product(product(coupler.T, inverse), coupler)
    following = jnp.zeros_like(shifted)
    real_parts = [None] * blocks
    imag_parts = [None] * blocks
    for block_index in reversed(range(blocks)):
        coupler = represent(coupling[block_index, 0], coupling[block_index, 1])
        inverse = greens[block_index]
        left_part = product(inverse, coupler)
        right_part = product(coupler.T, inverse)
        full_block = inverse + product(product(left_part, following), right_part)
        following = full_block
        pairs = pick_pairs(full_block, retained[block_index], orbitals)
        out_real, out_imag = correlate(pairs[0], pairs[1], pairs[2], pairs[3])
        real_parts[block_index] = out_real
        imag_parts[block_index] = out_imag
    return jnp.stack([jnp.stack(real_parts, axis=1), jnp.stack(imag_parts, axis=1)])
```

```python
import jax
import jax.numpy as jnp
from jax import lax
from jax.experimental import pallas as pl
from jax.experimental.pallas import tpu as pltpu
from jax.sharding import PartitionSpec as P

ORB = 128
BROADENING = 0.04
PANEL = 32
F32 = jnp.float32
CHAINS = 16


def product(left, right):
    return jnp.dot(left, right, precision=lax.Precision.HIGHEST, preferred_element_type=F32)


def rep(packed):
    real, imag = packed[:, :ORB], packed[:, ORB:]
    upper = jnp.concatenate([real, imag], axis=1)
    lower = jnp.concatenate([-imag, real], axis=1)
    return jnp.concatenate([upper, lower], axis=0)


def adjoint(packed):
    return jnp.concatenate([packed[:, :ORB].T, -packed[:, ORB:].T], axis=1)


def cmul(ar, ai, br, bi):
    return ar * br - ai * bi, ar * bi + ai * br


def lanes(x, j):
    return jnp.broadcast_to(x[..., j : j + 1], x.shape)


def sublanes(x3, k):
    tile = x3[k // 8]
    return jnp.take_along_axis(tile, jnp.full((8, 128), k % 8, jnp.int32), axis=0)


def panel_step(xr, xi, off):
    nb = xr.shape[0]
    shape = (nb, 8, 128)
    row = lax.broadcasted_iota(jnp.int32, shape, 0) * 8 + lax.broadcasted_iota(jnp.int32, shape, 1)
    lane = lax.broadcasted_iota(jnp.int32, shape, 2)
    lane1 = lane[0]
    for k in range(0, nb * 8, 2):
        j = off + k
        c0r, c0i, c1r, c1i = lanes(xr, j), lanes(xi, j), lanes(xr, j + 1), lanes(xi, j + 1)
        r0r, r0i = sublanes(xr, k), sublanes(xi, k)
        r1r, r1i = sublanes(xr, k + 1), sublanes(xi, k + 1)
        pr, pi = sublanes(c0r, k), sublanes(c0i, k)
        qr, qi = sublanes(c1r, k), sublanes(c1i, k)
        tr, ti = sublanes(c0r, k + 1), sublanes(c0i, k + 1)
        ur, ui = sublanes(c1r, k + 1), sublanes(c1i, k + 1)
        dr, di = cmul(pr, pi, ur, ui)
        er, ei = cmul(qr, qi, tr, ti)
        dr, di = dr - er, di - ei
        d = 1.0 / (dr * dr + di * di)
        m0, m1 = lane1 == j, lane1 == j + 1
        mm = m0 | m1
        r0r = jnp.where(m0, 1.0, jnp.where(m1, 0.0, r0r))
        r0i = jnp.where(mm, 0.0, r0i)
        r1r = jnp.where(m1, 1.0, jnp.where(m0, 0.0, r1r))
        r1i = jnp.where(mm, 0.0, r1i)
        ar, ai = cmul(ur, ui, r0r, r0i)
        br, bi = cmul(qr, qi, r1r, r1i)
        s0r, s0i = cmul(ar - br, ai - bi, dr, -di)
        ar, ai = cmul(pr, pi, r1r, r1i)
        br, bi = cmul(tr, ti, r0r, r0i)
        s1r, s1i = cmul(ar - br, ai - bi, dr, -di)
        k0, k1 = row == k, row == k + 1
        kk = k0 | k1
        z = kk | (lane == j) | (lane == j + 1)
        c0r = jnp.where(k0, -1.0, jnp.where(k1, 0.0, c0r))
        c0i = jnp.where(kk, 0.0, c0i)
        c1r = jnp.where(k1, -1.0, jnp.where(k0, 0.0, c1r))
        c1i = jnp.where(kk, 0.0, c1i)
        e0r, e0i = cmul(c0r, c0i, s0r, s0i)
        e1r, e1i = cmul(c1r, c1i, s1r, s1i)
        xr = jnp.where(z, 0.0, xr) - (e0r + e1r) * d
        xi = jnp.where(z, 0.0, xi) - (e0i + e1i) * d
    return xr, xi


def invert(packed, ar, ai):
    ar[...] = packed[:, :ORB]
    ai[...] = packed[:, ORB:]
    b = PANEL
    count = ORB // b
    lane = lax.broadcasted_iota(jnp.int32, (b, ORB), 1)
    for t in range(count):
        s = slice(t * b, (t + 1) * b)
        shape = (b // 8, 8, 128)
        xr, xi = panel_step(ar[s, :].reshape(shape), ai[s, :].reshape(shape), t * b)
        xr, xi = xr.reshape(b, ORB), xi.reshape(b, ORB)
        table = rep(jnp.concatenate([xr, xi], axis=1))
        inside = (lane >= t * b) & (lane < (t + 1) * b)
        for q in range(1, count):
            u = (t + q) % count
            other = slice(u * b, (u + 1) * b)
            column = jnp.concatenate([ar[other, s], ai[other, s]], axis=1)
            delta = product(column, table)
            ar[other, :] = jnp.where(inside, 0.0, ar[other, :]) - delta[:, :ORB]
            ai[other, :] = jnp.where(inside, 0.0, ai[other, :]) - delta[:, ORB:]
        ar[s, :] = xr
        ai[s, :] = xi
    return jnp.concatenate([ar[...], ai[...]], axis=1)


SCRATCH = [pltpu.VMEM((ORB, ORB), F32), pltpu.VMEM((ORB, ORB), F32)]
PACKED = jax.ShapeDtypeStruct((ORB, 2 * ORB), F32)
DOUBLE = jax.ShapeDtypeStruct((ORB, 4 * ORB), F32)
VM = pl.BlockSpec(memory_space=pltpu.VMEM)
SM = pl.BlockSpec(memory_space=pltpu.SMEM)


def first_kernel(scalars, onsite, coupling, diag_out, inverse_out, coupler_out, ar, ai):
    energy = scalars[0]
    last = scalars[1]
    row = lax.broadcasted_iota(jnp.int32, (ORB, ORB), 0)
    column = lax.broadcasted_iota(jnp.int32, (ORB, ORB), 1)
    eye = row == column
    raw_real, raw_imag = onsite[0, 0], onsite[0, 1]
    real = jnp.where(eye, energy, 0.0) - 0.5 * (raw_real + raw_real.T)
    imag = jnp.where(eye, BROADENING, 0.0) - 0.5 * (raw_imag - raw_imag.T)
    coupler = jnp.concatenate([coupling[0, 0], coupling[0, 1]], axis=1)
    diag_out[...] = jnp.concatenate([real, imag], axis=1)
    coupler_out[...] = -coupler

    @pl.when(last > 0.5)
    def contact():
        square = product(coupler, rep(adjoint(coupler)))
        diag_out[:, :ORB] = real - 0.5 * square[:, ORB:]
        diag_out[:, ORB:] = imag + 0.5 * square[:, :ORB]
        coupler_out[...] = jnp.zeros_like(coupler)

    inverse_out[...] = invert(diag_out[...], ar, ai)


def second_kernel(inverse, upper, previous, lower_out, send_out):
    lower = -adjoint(jnp.concatenate([previous[0, 0], previous[0, 1]], axis=1))
    lower_out[...] = lower
    send_out[:, : 2 * ORB] = product(inverse[...], rep(upper[...]))
    send_out[:, 2 * ORB :] = product(inverse[...], rep(lower))


def level_kernel(diag, lower, upper, left, right, diag_out, lower_out, upper_out, send_out, ar, ai):
    from_left = product(lower[...], rep(left[:, : 2 * ORB]))
    from_right = product(upper[...], rep(right[:, 2 * ORB :]))
    new_diag = diag[...] - from_left - from_right
    diag_out[...] = new_diag
    new_lower = -product(lower[...], rep(left[:, 2 * ORB :]))
    new_upper = -product(upper[...], rep(right[:, : 2 * ORB]))
    lower_out[...] = new_lower
    upper_out[...] = new_upper
    inverse = invert(new_diag, ar, ai)
    send_out[:, : 2 * ORB] = product(inverse, rep(new_upper))
    send_out[:, 2 * ORB :] = product(inverse, rep(new_lower))


def fourth_kernel(diag, lower, upper, left, right, diag_out, across_out, send_out, ar, ai):
    from_left = product(lower[...], rep(left[:, : 2 * ORB]))
    from_right = product(upper[...], rep(right[:, 2 * ORB :]))
    new_diag = diag[...] - from_left - from_right
    diag_out[...] = new_diag
    new_lower = -product(lower[...], rep(left[:, 2 * ORB :]))
    new_upper = -product(upper[...], rep(right[:, : 2 * ORB]))
    across = new_lower + new_upper
    across_out[...] = across
    inverse = invert(new_diag, ar, ai)
    send_out[...] = product(inverse, rep(across))


def last_kernel(diag, across, partner, retained, out, ar, ai):
    green = invert(diag[...] - product(across[...], rep(partner[...])), ar, ai)
    turned = jnp.concatenate([green[:, :ORB].T, green[:, ORB:].T], axis=0)
    high = turned.astype(jnp.bfloat16)
    rest = turned - high.astype(F32)
    middle = rest.astype(jnp.bfloat16)
    table = jnp.concatenate([high, middle], axis=1)
    rows = lax.broadcasted_iota(jnp.int32, (ORB, 256), 0)

    def chunk(step, carry):
        index = retained[0:1, pl.ds(pl.multiple_of(step * 256, 256), 256)]
        first = rows == (index >> 7)
        second = rows == (index & 127)
        hot_first = jnp.where(first, 1.0, 0.0).astype(jnp.bfloat16)
        hot_second = jnp.where(second, 1.0, 0.0).astype(jnp.bfloat16)
        direct = jnp.dot(
            table, jnp.concatenate([hot_first, hot_first], axis=0), preferred_element_type=F32
        )
        mirror = jnp.dot(
            table, jnp.concatenate([hot_second, hot_second], axis=0), preferred_element_type=F32
        )
        parts = [
            jnp.where(second, direct[:ORB], 0.0),
            jnp.where(second, direct[ORB:], 0.0),
            jnp.where(first, mirror[:ORB], 0.0),
            jnp.where(first, mirror[ORB:], 0.0),
        ]
        sums = [jnp.sum(part, axis=0, keepdims=True) for part in parts]
        tile = []
        for value in sums:
            tile += [value[:, :128], value[:, 128:]]
        out[step] = jnp.concatenate(tile, axis=0)
        return carry

    lax.fori_loop(0, 32, chunk, 0)


def correlate_kernel(received, out, second_real, second_imag):
    for half in range(2):
        s = slice(half * 128, (half + 1) * 128)
        ar = received[pl.ds(0 + half, 32, stride=8), :]
        ai = received[pl.ds(2 + half, 32, stride=8), :]
        br = received[pl.ds(4 + half, 32, stride=8), :]
        bi = received[pl.ds(6 + half, 32, stride=8), :]
        second_real[0:32, :] = br
        second_real[32:64, :] = br
        second_imag[0:32, :] = bi
        second_imag[32:64, :] = bi
        total_real = jnp.zeros((32, 128), F32)
        total_imag = jnp.zeros((32, 128), F32)
        for n in range(32):
            xr = jnp.broadcast_to(ar[n : n + 1, :], (32, 128))
            xi = jnp.broadcast_to(ai[n : n + 1, :], (32, 128))
            yr = second_real[n : n + 32, :]
            yi = second_imag[n : n + 32, :]
            pr, pi = cmul(xr, xi, yr, yi)
            total_real += pr
            total_imag += pi
        out[0, :, s] = total_real
        out[1, :, s] = total_imag


def green_pairs(onsite, coupling, retained, energy):
    position = lax.axis_index("chain")
    scalars = jnp.stack([energy, (position == CHAINS - 1).astype(F32)])

    def moved(value, by):
        pairs = [(i, i + by) for i in range(CHAINS) if 0 <= i + by < CHAINS]
        return lax.ppermute(value, "chain", pairs)

    previous = moved(coupling, 1)
    diag, inverse, upper = pl.pallas_call(
        first_kernel,
        in_specs=[SM, VM, VM],
        out_shape=[PACKED, PACKED, PACKED],
        scratch_shapes=SCRATCH,
    )(scalars, onsite, coupling)
    lower, send = pl.pallas_call(second_kernel, out_shape=[PACKED, DOUBLE])(
        inverse, upper, previous
    )
    for distance in (1, 2):
        left = moved(send, distance)
        right = moved(send, -distance)
        diag, lower, upper, send = pl.pallas_call(
            level_kernel,
            out_shape=[PACKED, PACKED, PACKED, DOUBLE],
            scratch_shapes=SCRATCH,
        )(diag, lower, upper, left, right)
    left = moved(send, 4)
    right = moved(send, -4)
    diag, across, send = pl.pallas_call(
        fourth_kernel,
        out_shape=[PACKED, PACKED, PACKED],
        scratch_shapes=SCRATCH,
    )(diag, lower, upper, left, right)
    partner = lax.ppermute(send, "chain", [(i, (i + 8) % CHAINS) for i in range(CHAINS)])
    return pl.pallas_call(
        last_kernel,
        out_shape=jax.ShapeDtypeStruct((32, 8, 128), F32),
        scratch_shapes=SCRATCH,
    )(diag, across, partner, retained)


def correlate(received):
    result = pl.pallas_call(
        correlate_kernel,
        out_shape=jax.ShapeDtypeStruct((2, 32, 256), F32),
        scratch_shapes=[pltpu.VMEM((64, 128), F32), pltpu.VMEM((64, 128), F32)],
    )(received.reshape(256, 128))
    return result.reshape(2, 32, 1, 256)


def shards(onsite, coupling, retained):
    groups = lax.axis_size("energy")
    energy = -2.0 + 4.0 * lax.axis_index("energy").astype(F32) / groups
    gathered = green_pairs(onsite, coupling, retained, energy)
    received = lax.all_to_all(gathered, "energy", split_axis=0, concat_axis=0, tiled=True)
    return correlate(received)


def solution(mesh):
    in_specs = (P("chain", None, None, None), P("chain", None, None, None), P("chain", None))
    out_specs = P(None, None, "chain", "energy")
    return jax.shard_map(shards, mesh=mesh, in_specs=in_specs, out_specs=out_specs, check_vma=False)
```

```python
import jax
import jax.numpy as jnp
from jax import lax
from jax.experimental import pallas as pl
from jax.experimental.pallas import tpu as pltpu
from jax.sharding import PartitionSpec as P

ORB = 128
BROADENING = 0.04
PANEL = 32
UNROLL = 4
F32 = jnp.float32
CHAINS = 16


def product(left, right):
    return jnp.dot(left, right, precision=lax.Precision.HIGHEST, preferred_element_type=F32)


def rep(packed):
    real, imag = packed[:, :ORB], packed[:, ORB:]
    upper = jnp.concatenate([real, imag], axis=1)
    lower = jnp.concatenate([-imag, real], axis=1)
    return jnp.concatenate([upper, lower], axis=0)


def adjoint(packed):
    return jnp.concatenate([packed[:, :ORB].T, -packed[:, ORB:].T], axis=1)


def cmul(a, b):
    return a[0] * b[0] - a[1] * b[1], a[0] * b[1] + a[1] * b[0]


def cadd(a, b):
    return a[0] + b[0], a[1] + b[1]


def lanes(x, j):
    return jnp.broadcast_to(x[..., j : j + 1], x.shape)


def sublanes(tile, k):
    return jnp.take_along_axis(tile, jnp.full((8, 128), k, jnp.int32), axis=0)


def pivots(real, imag, own, others):
    lane = lax.broadcasted_iota(jnp.int32, (8, 128), 1)
    row = lax.broadcasted_iota(jnp.int32, (8, 128), 0)
    j = 8 * own
    cols = {
        u: [(lanes(real[u], j + c), lanes(imag[u], j + c)) for c in range(8)]
        for u in [own] + others
    }
    ahead = list(cols[own])
    whole = (real[own], imag[own])
    for a in range(8):
        pr, pi = sublanes(ahead[a][0], a), sublanes(ahead[a][1], a)
        scale = 1.0 / (pr * pr + pi * pi)
        is_row = row == a
        factor = (jnp.where(is_row, -1.0, ahead[a][0]), jnp.where(is_row, 0.0, ahead[a][1]))

        def eliminate(y, is_col):
            er, ei = sublanes(y[0], a), sublanes(y[1], a)
            br, bi = jnp.where(is_row, 0.0, y[0]), jnp.where(is_row, 0.0, y[1])
            if is_col is not None:
                er, ei = jnp.where(is_col, 1.0, er), jnp.where(is_col, 0.0, ei)
                br, bi = jnp.where(is_col, 0.0, br), jnp.where(is_col, 0.0, bi)
            scaled = cmul(factor, (er * pr + ei * pi, ei * pr - er * pi))
            return br - scaled[0] * scale, bi - scaled[1] * scale

        for c in range(a + 1, 8):
            ahead[c] = eliminate(ahead[c], None)
        whole = eliminate(whole, lane == j + a)
    real[own], imag[own] = whole
    rows = [(sublanes(whole[0], c), sublanes(whole[1], c)) for c in range(8)]
    inside = (lane >= j) & (lane < j + 8)
    for u in others:
        terms = [cmul(cols[u][c], rows[c]) for c in range(8)]
        while len(terms) > 1:
            terms = [cadd(terms[2 * q], terms[2 * q + 1]) for q in range(len(terms) // 2)]
        real[u] = jnp.where(inside, 0.0, real[u]) - terms[0][0]
        imag[u] = jnp.where(inside, 0.0, imag[u]) - terms[0][1]


def invert(matrix):
    count, extra = ORB // 8, 2
    panel = PANEL // 8
    lane = lax.broadcasted_iota(jnp.int32, (8, 128), 1)
    real = [matrix[8 * u : 8 * u + 8, :ORB] for u in range(count)]
    imag = [matrix[8 * u : 8 * u + 8, ORB:] for u in range(count)]
    for start in range(0, count, panel):
        own = list(range(start, start + panel))
        soon = list(range(start + panel, min(start + panel + extra, count)))
        rest = [u % count for u in range(start + panel, start + count)]
        rest = [u for u in rest if u not in soon]
        s = slice(8 * start, 8 * start + PANEL)
        col_real = {u: real[u][:, s] for u in rest}
        col_imag = {u: imag[u][:, s] for u in rest}
        for q, t in enumerate(own):
            pivots(real, imag, t, own[q + 1 :] + soon + own[:q])
        table = rep(
            jnp.concatenate(
                [
                    jnp.concatenate([real[u] for u in own], axis=0),
                    jnp.concatenate([imag[u] for u in own], axis=0),
                ],
                axis=1,
            )
        )
        inside = (lane >= 8 * start) & (lane < 8 * start + PANEL)
        cut = panel - extra if soon else len(rest)
        for chunk in (rest[:cut], rest[cut:]):
            if chunk:
                sides = [
                    jnp.concatenate([col_real[u] for u in chunk], axis=0),
                    jnp.concatenate([col_imag[u] for u in chunk], axis=0),
                ]
                delta = product(jnp.concatenate(sides, axis=1), table)
                for n, u in enumerate(chunk):
                    part = delta[8 * n : 8 * n + 8]
                    real[u] = jnp.where(inside, 0.0, real[u]) - part[:, :ORB]
                    imag[u] = jnp.where(inside, 0.0, imag[u]) - part[:, ORB:]
    return jnp.concatenate(
        [jnp.concatenate(real, axis=0), jnp.concatenate(imag, axis=0)], axis=1
    )


PACKED = jax.ShapeDtypeStruct((ORB, 2 * ORB), F32)
DOUBLE = jax.ShapeDtypeStruct((ORB, 4 * ORB), F32)
VM = pl.BlockSpec(memory_space=pltpu.VMEM)
SM = pl.BlockSpec(memory_space=pltpu.SMEM)
W = 2 * ORB


def packed(raw):
    return jnp.concatenate([raw[0, 0], raw[0, 1]], axis=1)


def first_kernel(scalars, onsite, coupling, diag_out, upper_out, even_out, odd_out):
    energy = scalars[0]
    row = lax.broadcasted_iota(jnp.int32, (ORB, ORB), 0)
    column = lax.broadcasted_iota(jnp.int32, (ORB, ORB), 1)
    eye = row == column
    raw_real, raw_imag = onsite[0, 0], onsite[0, 1]
    real = jnp.where(eye, energy, 0.0) - 0.5 * (raw_real + raw_real.T)
    imag = jnp.where(eye, BROADENING, 0.0) - 0.5 * (raw_imag - raw_imag.T)
    diag_out[...] = jnp.concatenate([real, imag], axis=1)
    upper_out[...] = packed(coupling)

    @pl.when(scalars[1] > 0.5)
    def contact():
        coupler = packed(coupling)
        square = product(coupler, rep(adjoint(coupler)))
        diag_out[:, :ORB] = real - 0.5 * square[:, ORB:]
        diag_out[:, ORB:] = imag + 0.5 * square[:, :ORB]
        upper_out[...] = jnp.zeros_like(coupler)

    inverse = invert(diag_out[...])
    upper = upper_out[...]
    table = rep(upper)
    onward = product(adjoint(upper), rep(inverse))
    up = jnp.concatenate([product(onward, table), onward], axis=1)
    down = jnp.concatenate([inverse, product(inverse, table)], axis=1)
    even = scalars[2] > 0.5

    @pl.when(even)
    def store_even():
        even_out[...] = up
        odd_out[...] = down

    @pl.when(jnp.logical_not(even))
    def store_odd():
        even_out[...] = down
        odd_out[...] = up


def second_kernel(
    scalars, diag, coupler, before, even_in, odd_in, diag_out, lower_out, upper_out, send_out
):
    even = scalars[2] > 0.5
    left = jnp.where(even, odd_in[...], even_in[...])
    right = jnp.where(even, even_in[...], odd_in[...])
    upper = coupler[...]
    from_right = product(product(upper, rep(right[:, :W])), rep(adjoint(upper)))
    new_diag = diag[...] - left[:, :W] - from_right
    diag_out[...] = new_diag
    new_lower = -product(left[:, W:], rep(adjoint(packed(before))))
    new_upper = -product(upper, rep(right[:, W:]))
    lower_out[...] = new_lower
    upper_out[...] = new_upper
    inverse = invert(new_diag)
    send_out[:, :W] = product(inverse, rep(new_upper))
    send_out[:, W:] = product(inverse, rep(new_lower))


def folded(diag, lower, upper, left, right):
    sides = jnp.concatenate([lower[...], upper[...]], axis=1)
    tables = jnp.concatenate([rep(left[:, :W]), rep(right[:, W:])], axis=0)
    return diag[...] - product(sides, tables)


def third_kernel(diag, lower, upper, left, right, diag_out, lower_out, upper_out, send_out):
    new_diag = folded(diag, lower, upper, left, right)
    diag_out[...] = new_diag
    new_lower = -product(lower[...], rep(left[:, W:]))
    new_upper = -product(upper[...], rep(right[:, :W]))
    lower_out[...] = new_lower
    upper_out[...] = new_upper
    inverse = invert(new_diag)
    send_out[:, :W] = product(inverse, rep(new_upper))
    send_out[:, W:] = product(inverse, rep(new_lower))


def fourth_kernel(diag, lower, upper, left, right, diag_out, across_out, send_out):
    new_diag = folded(diag, lower, upper, left, right)
    diag_out[...] = new_diag
    sides = jnp.concatenate([lower[...], upper[...]], axis=1)
    tables = jnp.concatenate([rep(left[:, W:]), rep(right[:, :W])], axis=0)
    across = -product(sides, tables)
    across_out[...] = across
    inverse = invert(new_diag)
    send_out[...] = product(inverse, rep(across))


def last_kernel(diag, across, partner, retained, out):
    green = invert(diag[...] - product(across[...], rep(partner[...])))
    real, imag = green[:, :ORB], green[:, ORB:]
    stack = jnp.concatenate([real.T, imag.T, real, imag], axis=0)
    high = stack.astype(jnp.bfloat16)
    middle = (stack - high.astype(F32)).astype(jnp.bfloat16)
    table = jnp.concatenate([high, middle], axis=1)
    rows = lax.broadcasted_iota(jnp.int32, (ORB, 256), 0)

    def chunk(step, carry):
        index = retained[0:1, pl.ds(pl.multiple_of(step * 256, 256), 256)]
        first = rows == (index >> 7)
        second = rows == (index & 127)
        hot = jnp.where(first, 1.0, 0.0).astype(jnp.bfloat16)
        picked = jnp.dot(
            table, jnp.concatenate([hot, hot], axis=0), preferred_element_type=F32
        )
        tile = []
        for part in range(4):
            chosen = jnp.where(second, picked[part * ORB : (part + 1) * ORB], 0.0)
            partial = jnp.sum(chosen.reshape(16, 8, 256), axis=0)
            for half in range(2):
                piece = partial[:, half * 128 : (half + 1) * 128]
                tile.append(jnp.sum(piece, axis=0, keepdims=True))
        out[step] = jnp.concatenate(tile, axis=0)
        return carry

    lax.fori_loop(0, 32, chunk, 0, unroll=UNROLL)


def correlate_kernel(received, out, second_real, second_imag):
    for half in range(2):
        s = slice(half * 128, (half + 1) * 128)
        ar = received[pl.ds(0 + half, 32, stride=8), :]
        ai = received[pl.ds(2 + half, 32, stride=8), :]
        br = received[pl.ds(4 + half, 32, stride=8), :]
        bi = received[pl.ds(6 + half, 32, stride=8), :]
        second_real[0:32, :] = br
        second_real[32:64, :] = br
        second_imag[0:32, :] = bi
        second_imag[32:64, :] = bi
        total_real = jnp.zeros((32, 128), F32)
        total_imag = jnp.zeros((32, 128), F32)
        for n in range(32):
            x = (
                jnp.broadcast_to(ar[n : n + 1, :], (32, 128)),
                jnp.broadcast_to(ai[n : n + 1, :], (32, 128)),
            )
            term = cmul(x, (second_real[n : n + 32, :], second_imag[n : n + 32, :]))
            total_real += term[0]
            total_imag += term[1]
        out[0, :, 0, s] = total_real
        out[1, :, 0, s] = total_imag


def green_pairs(onsite, coupling, retained, energy):
    position = lax.axis_index("chain")
    last = (position == CHAINS - 1).astype(F32)
    even = (position % 2 == 0).astype(F32)
    scalars = jnp.stack([energy, last, even])

    def moved(value, by):
        pairs = [(i, i + by) for i in range(CHAINS) if 0 <= i + by < CHAINS]
        return lax.ppermute(value, "chain", pairs)

    def swapped(value, start):
        pairs = [(i, i + 1) for i in range(start, CHAINS - 1, 2)]
        return lax.ppermute(value, "chain", pairs + [(b, a) for a, b in pairs])

    before = moved(coupling, 2)
    diag, upper, even_send, odd_send = pl.pallas_call(
        first_kernel,
        in_specs=[SM, VM, VM],
        out_shape=[PACKED, PACKED, DOUBLE, DOUBLE],
    )(scalars, onsite, coupling)
    before, even_send, odd_send = lax.optimization_barrier((before, even_send, odd_send))
    even_in = swapped(even_send, 0)
    odd_in = swapped(odd_send, 1)
    diag, lower, upper, send = pl.pallas_call(
        second_kernel,
        in_specs=[SM] + [VM] * 5,
        out_shape=[PACKED, PACKED, PACKED, DOUBLE],
    )(scalars, diag, upper, before, even_in, odd_in)
    left = moved(send, 2)
    right = moved(send, -2)
    diag, lower, upper, send = pl.pallas_call(
        third_kernel,
        out_shape=[PACKED, PACKED, PACKED, DOUBLE],
    )(diag, lower, upper, left, right)
    left = moved(send, 4)
    right = moved(send, -4)
    diag, across, send = pl.pallas_call(
        fourth_kernel,
        out_shape=[PACKED, PACKED, PACKED],
    )(diag, lower, upper, left, right)
    partner = lax.ppermute(send, "chain", [(i, (i + 8) % CHAINS) for i in range(CHAINS)])
    return pl.pallas_call(
        last_kernel,
        out_shape=jax.ShapeDtypeStruct((32, 8, 128), F32),
    )(diag, across, partner, retained)


def correlate(received):
    return pl.pallas_call(
        correlate_kernel,
        out_shape=jax.ShapeDtypeStruct((2, 32, 1, 256), F32),
        scratch_shapes=[pltpu.VMEM((64, 128), F32), pltpu.VMEM((64, 128), F32)],
    )(received.reshape(256, 128))


def shards(onsite, coupling, retained):
    groups = lax.axis_size("energy")
    energy = -2.0 + 4.0 * lax.axis_index("energy").astype(F32) / groups
    gathered = green_pairs(onsite, coupling, retained, energy)
    received = lax.all_to_all(gathered, "energy", split_axis=0, concat_axis=0, tiled=True)
    return correlate(received)


def solution(mesh):
    in_specs = (P("chain", None, None, None), P("chain", None, None, None), P("chain", None))
    out_specs = P(None, None, "chain", "energy")
    return jax.shard_map(shards, mesh=mesh, in_specs=in_specs, out_specs=out_specs, check_vma=False)
```

```python
import jax
import jax.numpy as jnp
from jax import lax
from jax.experimental import pallas as pl
from jax.experimental.pallas import tpu as pltpu
from jax.sharding import PartitionSpec as P

ORB = 128
BROADENING = 0.04
PANEL = 32
UNROLL = 4
F32 = jnp.float32
CHAINS = 16


def product(left, right):
    return jnp.dot(left, right, precision=lax.Precision.HIGHEST, preferred_element_type=F32)


def rep(packed):
    real, imag = packed[:, :ORB], packed[:, ORB:]
    upper = jnp.concatenate([real, imag], axis=1)
    lower = jnp.concatenate([-imag, real], axis=1)
    return jnp.concatenate([upper, lower], axis=0)


def adjoint(packed):
    return jnp.concatenate([packed[:, :ORB].T, -packed[:, ORB:].T], axis=1)


def cmul(a, b):
    return a[0] * b[0] - a[1] * b[1], a[0] * b[1] + a[1] * b[0]


def cadd(a, b):
    return a[0] + b[0], a[1] + b[1]


def lanes(x, j):
    return jnp.broadcast_to(x[..., j : j + 1], x.shape)


def sublanes(tile, k):
    return jnp.take_along_axis(tile, jnp.full((8, 128), k, jnp.int32), axis=0)


def pivots(real, imag, own, others):
    lane = lax.broadcasted_iota(jnp.int32, (8, 128), 1)
    row = lax.broadcasted_iota(jnp.int32, (8, 128), 0)
    j = 8 * own
    cols = {
        u: [(lanes(real[u], j + c), lanes(imag[u], j + c)) for c in range(8)]
        for u in [own] + others
    }
    ahead = list(cols[own])
    whole = (real[own], imag[own])
    for a in range(8):
        pr, pi = sublanes(ahead[a][0], a), sublanes(ahead[a][1], a)
        scale = 1.0 / (pr * pr + pi * pi)
        is_row = row == a
        factor = (jnp.where(is_row, -1.0, ahead[a][0]), jnp.where(is_row, 0.0, ahead[a][1]))
        factor = cmul(factor, (pr, -pi))

        def eliminate(y, is_col):
            er, ei = sublanes(y[0], a), sublanes(y[1], a)
            br, bi = jnp.where(is_row, 0.0, y[0]), jnp.where(is_row, 0.0, y[1])
            if is_col is not None:
                er, ei = jnp.where(is_col, 1.0, er), jnp.where(is_col, 0.0, ei)
                br, bi = jnp.where(is_col, 0.0, br), jnp.where(is_col, 0.0, bi)
            scaled = cmul(factor, (er, ei))
            return br - scaled[0] * scale, bi - scaled[1] * scale

        for c in range(a + 1, 8):
            ahead[c] = eliminate(ahead[c], None)
        whole = eliminate(whole, lane == j + a)
    real[own], imag[own] = whole
    rows = [(sublanes(whole[0], c), sublanes(whole[1], c)) for c in range(8)]
    inside = (lane >= j) & (lane < j + 8)
    for u in others:
        terms = [cmul(cols[u][c], rows[c]) for c in range(8)]
        while len(terms) > 1:
            terms = [cadd(terms[2 * q], terms[2 * q + 1]) for q in range(len(terms) // 2)]
        real[u] = jnp.where(inside, 0.0, real[u]) - terms[0][0]
        imag[u] = jnp.where(inside, 0.0, imag[u]) - terms[0][1]


def invert(matrix):
    count, extra = ORB // 8, 2
    panel = PANEL // 8
    lane = lax.broadcasted_iota(jnp.int32, (8, 128), 1)
    real = [matrix[8 * u : 8 * u + 8, :ORB] for u in range(count)]
    imag = [matrix[8 * u : 8 * u + 8, ORB:] for u in range(count)]
    for start in range(0, count, panel):
        own = list(range(start, start + panel))
        soon = list(range(start + panel, min(start + panel + extra, count)))
        rest = [u % count for u in range(start + panel, start + count)]
        rest = [u for u in rest if u not in soon]
        s = slice(8 * start, 8 * start + PANEL)
        col_real = {u: real[u][:, s] for u in rest}
        col_imag = {u: imag[u][:, s] for u in rest}
        for q, t in enumerate(own):
            pivots(real, imag, t, own[q + 1 :] + soon + own[:q])
        table = rep(
            jnp.concatenate(
                [
                    jnp.concatenate([real[u] for u in own], axis=0),
                    jnp.concatenate([imag[u] for u in own], axis=0),
                ],
                axis=1,
            )
        )
        inside = (lane >= 8 * start) & (lane < 8 * start + PANEL)
        cut = panel - extra if soon else len(rest)
        for chunk in (rest[:cut], rest[cut:]):
            if chunk:
                sides = [
                    jnp.concatenate([col_real[u] for u in chunk], axis=0),
                    jnp.concatenate([col_imag[u] for u in chunk], axis=0),
                ]
                delta = product(jnp.concatenate(sides, axis=1), table)
                for n, u in enumerate(chunk):
                    part = delta[8 * n : 8 * n + 8]
                    real[u] = jnp.where(inside, 0.0, real[u]) - part[:, :ORB]
                    imag[u] = jnp.where(inside, 0.0, imag[u]) - part[:, ORB:]
    return jnp.concatenate(
        [jnp.concatenate(real, axis=0), jnp.concatenate(imag, axis=0)], axis=1
    )


PACKED = pltpu.VMEM((ORB, 2 * ORB), F32)
DOUBLE = pltpu.VMEM((ORB, 4 * ORB), F32)
VM = pl.BlockSpec(memory_space=pltpu.VMEM)
W = 2 * ORB


def packed(raw):
    return jnp.concatenate([raw[0, 0], raw[0, 1]], axis=1)


def first_kernel(onsite, coupling, diag_out, upper_out, even_out, odd_out):
    position = lax.axis_index("chain")
    energy = -2.0 + 4.0 * lax.axis_index("energy").astype(F32) / lax.axis_size("energy")
    row = lax.broadcasted_iota(jnp.int32, (ORB, ORB), 0)
    column = lax.broadcasted_iota(jnp.int32, (ORB, ORB), 1)
    eye = row == column
    raw_real, raw_imag = onsite[0, 0], onsite[0, 1]
    real = jnp.where(eye, energy, 0.0) - 0.5 * (raw_real + raw_real.T)
    imag = jnp.where(eye, BROADENING, 0.0) - 0.5 * (raw_imag - raw_imag.T)
    diag_out[...] = jnp.concatenate([real, imag], axis=1)
    upper_out[...] = packed(coupling)

    @pl.when(position == CHAINS - 1)
    def contact():
        coupler = packed(coupling)
        square = product(coupler, rep(adjoint(coupler)))
        diag_out[:, :ORB] = real - 0.5 * square[:, ORB:]
        diag_out[:, ORB:] = imag + 0.5 * square[:, :ORB]
        upper_out[...] = jnp.zeros_like(coupler)

    inverse = invert(diag_out[...])
    upper = upper_out[...]
    table = rep(upper)
    onward = product(adjoint(upper), rep(inverse))
    up = jnp.concatenate([product(onward, table), onward], axis=1)
    down = jnp.concatenate([inverse, product(inverse, table)], axis=1)
    even = position % 2 == 0

    @pl.when(even)
    def store_even():
        even_out[...] = up
        odd_out[...] = down

    @pl.when(jnp.logical_not(even))
    def store_odd():
        even_out[...] = down
        odd_out[...] = up


def second_kernel(
    diag, coupler, before, odd_in, even_in, diag_out, lower_out, upper_out, send_out
):
    even = lax.axis_index("chain") % 2 == 0
    left = jnp.where(even, odd_in[...], even_in[...])
    right = jnp.where(even, even_in[...], odd_in[...])
    upper = coupler[...]
    from_right = product(product(upper, rep(right[:, :W])), rep(adjoint(upper)))
    new_diag = diag[...] - left[:, :W] - from_right
    diag_out[...] = new_diag
    new_lower = -product(left[:, W:], rep(adjoint(packed(before))))
    new_upper = -product(upper, rep(right[:, W:]))
    lower_out[...] = new_lower
    upper_out[...] = new_upper
    inverse = invert(new_diag)
    send_out[:, :W] = product(inverse, rep(new_upper))
    send_out[:, W:] = product(inverse, rep(new_lower))


def folded(diag, lower, upper, left, right):
    sides = jnp.concatenate([lower[...], upper[...]], axis=1)
    tables = jnp.concatenate([rep(left[:, :W]), rep(right[:, W:])], axis=0)
    return diag[...] - product(sides, tables)


def third_kernel(diag, lower, upper, left, right, diag_out, lower_out, upper_out, send_out):
    new_diag = folded(diag, lower, upper, left, right)
    diag_out[...] = new_diag
    new_lower = -product(lower[...], rep(left[:, W:]))
    new_upper = -product(upper[...], rep(right[:, :W]))
    lower_out[...] = new_lower
    upper_out[...] = new_upper
    inverse = invert(new_diag)
    send_out[:, :W] = product(inverse, rep(new_upper))
    send_out[:, W:] = product(inverse, rep(new_lower))


def fourth_kernel(diag, lower, upper, left, right, diag_out, across_out, send_out):
    new_diag = folded(diag, lower, upper, left, right)
    diag_out[...] = new_diag
    sides = jnp.concatenate([lower[...], upper[...]], axis=1)
    tables = jnp.concatenate([rep(left[:, W:]), rep(right[:, :W])], axis=0)
    across = -product(sides, tables)
    across_out[...] = across
    inverse = invert(new_diag)
    send_out[...] = product(inverse, rep(across))


def last_kernel(diag, across, partner, retained, out):
    green = invert(diag[...] - product(across[...], rep(partner[...])))
    real, imag = green[:, :ORB], green[:, ORB:]
    stack = jnp.concatenate([real.T, imag.T, real, imag], axis=0)
    high = stack.astype(jnp.bfloat16)
    middle = (stack - high.astype(F32)).astype(jnp.bfloat16)
    table = jnp.concatenate([high, middle], axis=1)
    rows = lax.broadcasted_iota(jnp.int32, (ORB, 256), 0)

    def chunk(step, carry):
        index = retained[0:1, pl.ds(pl.multiple_of(step * 256, 256), 256)]
        first = rows == (index >> 7)
        second = rows == (index & 127)
        hot = jnp.where(first, 1.0, 0.0).astype(jnp.bfloat16)
        picked = jnp.dot(
            table, jnp.concatenate([hot, hot], axis=0), preferred_element_type=F32
        )
        tile = []
        for part in range(4):
            chosen = jnp.where(second, picked[part * ORB : (part + 1) * ORB], 0.0)
            partial = jnp.sum(chosen.reshape(16, 8, 256), axis=0)
            for half in range(2):
                piece = partial[:, half * 128 : (half + 1) * 128]
                tile.append(jnp.sum(piece, axis=0, keepdims=True))
        out[step] = jnp.concatenate(tile, axis=0)
        return carry

    lax.fori_loop(0, 32, chunk, 0, unroll=UNROLL)


def correlate_kernel(received, out, second_real, second_imag):
    for half in range(2):
        s = slice(half * 128, (half + 1) * 128)
        ar = received[pl.ds(0 + half, 32, stride=8), :]
        ai = received[pl.ds(2 + half, 32, stride=8), :]
        br = received[pl.ds(4 + half, 32, stride=8), :]
        bi = received[pl.ds(6 + half, 32, stride=8), :]
        second_real[0:32, :] = br
        second_real[32:64, :] = br
        second_imag[0:32, :] = bi
        second_imag[32:64, :] = bi
        total_real = jnp.zeros((32, 128), F32)
        total_imag = jnp.zeros((32, 128), F32)
        for n in range(32):
            x = (
                jnp.broadcast_to(ar[n : n + 1, :], (32, 128)),
                jnp.broadcast_to(ai[n : n + 1, :], (32, 128)),
            )
            term = cmul(x, (second_real[n : n + 32, :], second_imag[n : n + 32, :]))
            total_real += term[0]
            total_imag += term[1]
        out[0, :, 0, s] = total_real
        out[1, :, 0, s] = total_imag


def near(*arrays):
    return [pltpu.with_memory_space_constraint(x, pltpu.VMEM) for x in arrays]


def green_pairs(onsite, coupling, retained):
    def moved(value, by):
        pairs = [(i, i + by) for i in range(CHAINS) if 0 <= i + by < CHAINS]
        return lax.ppermute(value, "chain", pairs)

    def swapped(value, start):
        pairs = [(i, i + 1) for i in range(start, CHAINS - 1, 2)]
        return lax.ppermute(value, "chain", pairs + [(b, a) for a, b in pairs])

    before = moved(coupling, 2)
    diag, upper, even_send, odd_send = pl.pallas_call(
        first_kernel,
        in_specs=[VM, VM],
        out_specs=[VM] * 4,
        out_shape=[PACKED, PACKED, DOUBLE, DOUBLE],
    )(onsite, coupling)
    before, even_send, odd_send = lax.optimization_barrier((before, even_send, odd_send))
    odd_in = swapped(odd_send, 1)
    even_in = swapped(even_send, 0)
    diag, lower, upper, send = pl.pallas_call(
        second_kernel,
        in_specs=[VM] * 5,
        out_specs=[VM] * 4,
        out_shape=[PACKED, PACKED, PACKED, DOUBLE],
    )(*near(diag, upper, before, odd_in, even_in))
    left = moved(send, 2)
    right = moved(send, -2)
    diag, lower, upper, send = pl.pallas_call(
        third_kernel,
        in_specs=[VM] * 5,
        out_specs=[VM] * 4,
        out_shape=[PACKED, PACKED, PACKED, DOUBLE],
    )(*near(diag, lower, upper, left, right))
    left = moved(send, 4)
    right = moved(send, -4)
    diag, across, send = pl.pallas_call(
        fourth_kernel,
        in_specs=[VM] * 5,
        out_specs=[VM] * 3,
        out_shape=[PACKED, PACKED, PACKED],
    )(*near(diag, lower, upper, left, right))
    partner = lax.ppermute(send, "chain", [(i, (i + 8) % CHAINS) for i in range(CHAINS)])
    return pl.pallas_call(
        last_kernel,
        in_specs=[VM] * 4,
        out_specs=VM,
        out_shape=pltpu.VMEM((32, 8, 128), F32),
    )(*near(diag, across, partner), retained)


def correlate(received):
    return pl.pallas_call(
        correlate_kernel,
        in_specs=[VM],
        out_shape=jax.ShapeDtypeStruct((2, 32, 1, 256), F32),
        scratch_shapes=[pltpu.VMEM((64, 128), F32), pltpu.VMEM((64, 128), F32)],
    )(*near(received.reshape(256, 128)))


def shards(onsite, coupling, retained):
    gathered = green_pairs(onsite, coupling, retained)
    received = lax.all_to_all(gathered, "energy", split_axis=0, concat_axis=0, tiled=True)
    return correlate(received)


def solution(mesh):
    in_specs = (P("chain", None, None, None), P("chain", None, None, None), P("chain", None))
    out_specs = P(None, None, "chain", "energy")
    return jax.shard_map(shards, mesh=mesh, in_specs=in_specs, out_specs=out_specs, check_vma=False)
```

```python
import jax
import jax.numpy as jnp
from jax import lax
from jax.experimental import pallas as pl
from jax.experimental.pallas import tpu as pltpu
from jax.sharding import PartitionSpec as P

ORB = 128
BROADENING = 0.04
PANEL = 32
UNROLL = 16
F32 = jnp.float32
CHAINS = 16


def product(left, right):
    return jnp.dot(left, right, precision=lax.Precision.HIGHEST, preferred_element_type=F32)


def rep(packed):
    real, imag = packed[:, :ORB], packed[:, ORB:]
    upper = jnp.concatenate([real, imag], axis=1)
    lower = jnp.concatenate([-imag, real], axis=1)
    return jnp.concatenate([upper, lower], axis=0)


def adjoint(packed):
    return jnp.concatenate([packed[:, :ORB].T, -packed[:, ORB:].T], axis=1)


def cmul(a, b):
    return a[0] * b[0] - a[1] * b[1], a[0] * b[1] + a[1] * b[0]


def cadd(a, b):
    return a[0] + b[0], a[1] + b[1]


def lanes(x, j):
    return jnp.broadcast_to(x[..., j : j + 1], x.shape)


def sublanes(tile, k):
    return jnp.take_along_axis(tile, jnp.full((8, 128), k, jnp.int32), axis=0)


def pivots(real, imag, own, others):
    lane = lax.broadcasted_iota(jnp.int32, (8, 128), 1)
    row = lax.broadcasted_iota(jnp.int32, (8, 128), 0)
    j = 8 * own
    cols = {
        u: [(lanes(real[u], j + c), lanes(imag[u], j + c)) for c in range(8)]
        for u in [own] + others
    }
    ahead = list(cols[own])
    whole = (real[own], imag[own])
    for a in range(8):
        pr, pi = sublanes(ahead[a][0], a), sublanes(ahead[a][1], a)
        scale = 1.0 / (pr * pr + pi * pi)
        is_row = row == a
        factor = (jnp.where(is_row, -1.0, ahead[a][0]), jnp.where(is_row, 0.0, ahead[a][1]))
        factor = cmul(factor, (pr, -pi))

        def eliminate(y, is_col):
            er, ei = sublanes(y[0], a), sublanes(y[1], a)
            br, bi = jnp.where(is_row, 0.0, y[0]), jnp.where(is_row, 0.0, y[1])
            if is_col is not None:
                er, ei = jnp.where(is_col, 1.0, er), jnp.where(is_col, 0.0, ei)
                br, bi = jnp.where(is_col, 0.0, br), jnp.where(is_col, 0.0, bi)
            scaled = cmul(factor, (er, ei))
            return br - scaled[0] * scale, bi - scaled[1] * scale

        for c in range(a + 1, 8):
            ahead[c] = eliminate(ahead[c], None)
        whole = eliminate(whole, lane == j + a)
    real[own], imag[own] = whole
    rows = [(sublanes(whole[0], c), sublanes(whole[1], c)) for c in range(8)]
    inside = (lane >= j) & (lane < j + 8)
    for u in others:
        terms = [cmul(cols[u][c], rows[c]) for c in range(8)]
        while len(terms) > 1:
            terms = [cadd(terms[2 * q], terms[2 * q + 1]) for q in range(len(terms) // 2)]
        real[u] = jnp.where(inside, 0.0, real[u]) - terms[0][0]
        imag[u] = jnp.where(inside, 0.0, imag[u]) - terms[0][1]


def invert(matrix):
    count, extra = ORB // 8, 2
    panel = PANEL // 8
    lane = lax.broadcasted_iota(jnp.int32, (8, 128), 1)
    real = [matrix[8 * u : 8 * u + 8, :ORB] for u in range(count)]
    imag = [matrix[8 * u : 8 * u + 8, ORB:] for u in range(count)]
    for start in range(0, count, panel):
        own = list(range(start, start + panel))
        soon = list(range(start + panel, min(start + panel + extra, count)))
        rest = [u % count for u in range(start + panel, start + count)]
        rest = [u for u in rest if u not in soon]
        s = slice(8 * start, 8 * start + PANEL)
        col_real = {u: real[u][:, s] for u in rest}
        col_imag = {u: imag[u][:, s] for u in rest}
        for q, t in enumerate(own):
            pivots(real, imag, t, own[q + 1 :] + soon + own[:q])
        table = rep(
            jnp.concatenate(
                [
                    jnp.concatenate([real[u] for u in own], axis=0),
                    jnp.concatenate([imag[u] for u in own], axis=0),
                ],
                axis=1,
            )
        )
        inside = (lane >= 8 * start) & (lane < 8 * start + PANEL)
        cut = panel - extra if soon else len(rest)
        for chunk in (rest[:cut], rest[cut:]):
            if chunk:
                sides = [
                    jnp.concatenate([col_real[u] for u in chunk], axis=0),
                    jnp.concatenate([col_imag[u] for u in chunk], axis=0),
                ]
                delta = product(jnp.concatenate(sides, axis=1), table)
                for n, u in enumerate(chunk):
                    part = delta[8 * n : 8 * n + 8]
                    real[u] = jnp.where(inside, 0.0, real[u]) - part[:, :ORB]
                    imag[u] = jnp.where(inside, 0.0, imag[u]) - part[:, ORB:]
    return jnp.concatenate(
        [jnp.concatenate(real, axis=0), jnp.concatenate(imag, axis=0)], axis=1
    )


PACKED = pltpu.VMEM((ORB, 2 * ORB), F32)
DOUBLE = pltpu.VMEM((ORB, 4 * ORB), F32)
VM = pl.BlockSpec(memory_space=pltpu.VMEM)
W = 2 * ORB


def packed(raw):
    return jnp.concatenate([raw[0, 0], raw[0, 1]], axis=1)


def first_kernel(onsite, coupling, diag_out, upper_out, even_out, odd_out):
    position = lax.axis_index("chain")
    energy = -2.0 + 4.0 * lax.axis_index("energy").astype(F32) / lax.axis_size("energy")
    row = lax.broadcasted_iota(jnp.int32, (ORB, ORB), 0)
    column = lax.broadcasted_iota(jnp.int32, (ORB, ORB), 1)
    eye = row == column
    raw_real, raw_imag = onsite[0, 0], onsite[0, 1]
    real = jnp.where(eye, energy, 0.0) - 0.5 * (raw_real + raw_real.T)
    imag = jnp.where(eye, BROADENING, 0.0) - 0.5 * (raw_imag - raw_imag.T)
    diag_out[...] = jnp.concatenate([real, imag], axis=1)
    upper_out[...] = packed(coupling)

    @pl.when(position == CHAINS - 1)
    def contact():
        coupler = packed(coupling)
        square = product(coupler, rep(adjoint(coupler)))
        diag_out[:, :ORB] = real - 0.5 * square[:, ORB:]
        diag_out[:, ORB:] = imag + 0.5 * square[:, :ORB]
        upper_out[...] = jnp.zeros_like(coupler)

    inverse = invert(diag_out[...])
    upper = upper_out[...]
    table = rep(upper)
    onward = product(adjoint(upper), rep(inverse))
    up = jnp.concatenate([product(onward, table), onward], axis=1)
    down = jnp.concatenate([inverse, product(inverse, table)], axis=1)
    even = position % 2 == 0

    @pl.when(even)
    def store_even():
        even_out[...] = up
        odd_out[...] = down

    @pl.when(jnp.logical_not(even))
    def store_odd():
        even_out[...] = down
        odd_out[...] = up


def second_kernel(
    diag, coupler, before, odd_in, even_in, diag_out, lower_out, upper_out, send_out
):
    even = lax.axis_index("chain") % 2 == 0
    left = jnp.where(even, odd_in[...], even_in[...])
    right = jnp.where(even, even_in[...], odd_in[...])
    upper = coupler[...]
    from_right = product(product(upper, rep(right[:, :W])), rep(adjoint(upper)))
    new_diag = diag[...] - left[:, :W] - from_right
    diag_out[...] = new_diag
    new_lower = -product(left[:, W:], rep(adjoint(packed(before))))
    new_upper = -product(upper, rep(right[:, W:]))
    lower_out[...] = new_lower
    upper_out[...] = new_upper
    inverse = invert(new_diag)
    send_out[:, :W] = product(inverse, rep(new_upper))
    send_out[:, W:] = product(inverse, rep(new_lower))


def third_kernel(
    diag, lower, upper, left, right, diag_out, lower_out, upper_out, upward_out, downward_out
):
    sides = jnp.concatenate([lower[...], upper[...]], axis=1)
    tables = jnp.concatenate([rep(left[:, :W]), rep(right[:, W:])], axis=0)
    new_diag = diag[...] - product(sides, tables)
    diag_out[...] = new_diag
    new_lower = -product(lower[...], rep(left[:, W:]))
    new_upper = -product(upper[...], rep(right[:, :W]))
    lower_out[...] = new_lower
    upper_out[...] = new_upper
    inverse = invert(new_diag)
    upward_out[...] = product(inverse, rep(new_upper))
    downward_out[...] = product(inverse, rep(new_lower))


def fourth_kernel(diag, lower, upper, left, right, diag_out, side_out, send_out):
    sides = jnp.concatenate([lower[...], upper[...]], axis=1)
    tables = jnp.concatenate([rep(left[...]), rep(right[...])], axis=0)
    new_diag = diag[...] - product(sides, tables)
    diag_out[...] = new_diag
    side = jnp.where(lax.axis_index("chain") < CHAINS // 2, upper[...], lower[...])
    side_out[...] = side
    send_out[...] = product(invert(new_diag), rep(side))


def last_kernel(diag, side, left, right, left_late, right_late, partner, retained, out):
    low = lax.axis_index("chain") < CHAINS // 2
    outer = product(side[...], rep(left_late[...] + right_late[...]))
    near_side = jnp.where(low, right[...], left[...])
    inner = product(partner[...], rep(near_side))
    green = invert(diag[...] - product(outer, rep(inner)))
    real, imag = green[:, :ORB], green[:, ORB:]
    stack = jnp.concatenate([real.T, imag.T, real, imag], axis=0)
    high = stack.astype(jnp.bfloat16)
    middle = (stack - high.astype(F32)).astype(jnp.bfloat16)
    table = jnp.concatenate([high, middle], axis=1)
    rows = lax.broadcasted_iota(jnp.int32, (ORB, 256), 0)

    def chunk(step, carry):
        index = retained[0:1, pl.ds(pl.multiple_of(step * 256, 256), 256)]
        first = rows == (index >> 7)
        second = rows == (index & 127)
        hot = jnp.where(first, 1.0, 0.0).astype(jnp.bfloat16)
        picked = jnp.dot(
            table, jnp.concatenate([hot, hot], axis=0), preferred_element_type=F32
        )
        tile = []
        for part in range(4):
            chosen = jnp.where(second, picked[part * ORB : (part + 1) * ORB], 0.0)
            partial = jnp.sum(chosen.reshape(16, 8, 256), axis=0)
            for half in range(2):
                piece = partial[:, half * 128 : (half + 1) * 128]
                tile.append(jnp.sum(piece, axis=0, keepdims=True))
        out[step] = jnp.concatenate(tile, axis=0)
        return carry

    lax.fori_loop(0, 32, chunk, 0, unroll=UNROLL)


def correlate_kernel(received, out, second_real, second_imag):
    for half in range(2):
        s = slice(half * 128, (half + 1) * 128)
        ar = received[pl.ds(0 + half, 32, stride=8), :]
        ai = received[pl.ds(2 + half, 32, stride=8), :]
        br = received[pl.ds(4 + half, 32, stride=8), :]
        bi = received[pl.ds(6 + half, 32, stride=8), :]
        second_real[0:32, :] = br
        second_real[32:64, :] = br
        second_imag[0:32, :] = bi
        second_imag[32:64, :] = bi
        total_real = jnp.zeros((32, 128), F32)
        total_imag = jnp.zeros((32, 128), F32)
        for n in range(32):
            x = (
                jnp.broadcast_to(ar[n : n + 1, :], (32, 128)),
                jnp.broadcast_to(ai[n : n + 1, :], (32, 128)),
            )
            term = cmul(x, (second_real[n : n + 32, :], second_imag[n : n + 32, :]))
            total_real += term[0]
            total_imag += term[1]
        out[0, :, 0, s] = total_real
        out[1, :, 0, s] = total_imag


def near(*arrays):
    return [pltpu.with_memory_space_constraint(x, pltpu.VMEM) for x in arrays]


def green_pairs(onsite, coupling, retained):
    def moved(value, by):
        pairs = [(i, i + by) for i in range(CHAINS) if 0 <= i + by < CHAINS]
        return lax.ppermute(value, "chain", pairs)

    def swapped(value, start):
        pairs = [(i, i + 1) for i in range(start, CHAINS - 1, 2)]
        return lax.ppermute(value, "chain", pairs + [(b, a) for a, b in pairs])

    before = moved(coupling, 2)
    diag, upper, even_send, odd_send = pl.pallas_call(
        first_kernel,
        in_specs=[VM, VM],
        out_specs=[VM] * 4,
        out_shape=[PACKED, PACKED, DOUBLE, DOUBLE],
    )(onsite, coupling)
    before, even_send, odd_send = lax.optimization_barrier((before, even_send, odd_send))
    odd_in = swapped(odd_send, 1)
    even_in = swapped(even_send, 0)
    diag, lower, upper, send = pl.pallas_call(
        second_kernel,
        in_specs=[VM] * 5,
        out_specs=[VM] * 4,
        out_shape=[PACKED, PACKED, PACKED, DOUBLE],
    )(*near(diag, upper, before, odd_in, even_in))
    left = moved(send, 2)
    right = moved(send, -2)
    diag, lower, upper, upward, downward = pl.pallas_call(
        third_kernel,
        in_specs=[VM] * 5,
        out_specs=[VM] * 5,
        out_shape=[PACKED] * 5,
    )(*near(diag, lower, upper, left, right))
    left = moved(upward, 4)
    right = moved(downward, -4)
    middle = range(CHAINS // 4, 3 * CHAINS // 4)
    left_late = lax.ppermute(downward, "chain", [(i, i + 4) for i in middle])
    right_late = lax.ppermute(upward, "chain", [(i, i - 4) for i in middle])
    diag, side, send = pl.pallas_call(
        fourth_kernel,
        in_specs=[VM] * 5,
        out_specs=[VM] * 3,
        out_shape=[PACKED] * 3,
    )(*near(diag, lower, upper, left, right))
    send, left_late, right_late = lax.optimization_barrier((send, left_late, right_late))
    partner = lax.ppermute(send, "chain", [(i, (i + 8) % CHAINS) for i in range(CHAINS)])
    return pl.pallas_call(
        last_kernel,
        in_specs=[VM] * 8,
        out_specs=VM,
        out_shape=pltpu.VMEM((32, 8, 128), F32),
    )(*near(diag, side, left, right, left_late, right_late, partner), retained)


def correlate(received):
    return pl.pallas_call(
        correlate_kernel,
        in_specs=[VM],
        out_shape=jax.ShapeDtypeStruct((2, 32, 1, 256), F32),
        scratch_shapes=[pltpu.VMEM((64, 128), F32), pltpu.VMEM((64, 128), F32)],
    )(*near(received.reshape(256, 128)))


def shards(onsite, coupling, retained):
    gathered = green_pairs(onsite, coupling, retained)
    received = lax.all_to_all(gathered, "energy", split_axis=0, concat_axis=0, tiled=True)
    return correlate(received)


def solution(mesh):
    in_specs = (P("chain", None, None, None), P("chain", None, None, None), P("chain", None))
    out_specs = P(None, None, "chain", "energy")
    return jax.shard_map(shards, mesh=mesh, in_specs=in_specs, out_specs=out_specs, check_vma=False)
```

```python
import jax
import jax.numpy as jnp
from jax import lax
from jax.experimental import pallas as pl
from jax.experimental.pallas import tpu as pltpu
from jax.sharding import PartitionSpec as P

ORB = 128
BROADENING = 0.04
PANEL = 32
UNROLL = 16
F32 = jnp.float32
CHAINS = 16


def product(left, right):
    return jnp.dot(left, right, precision=lax.Precision.HIGHEST, preferred_element_type=F32)


def rep(packed):
    real, imag = packed[:, :ORB], packed[:, ORB:]
    upper = jnp.concatenate([real, imag], axis=1)
    lower = jnp.concatenate([-imag, real], axis=1)
    return jnp.concatenate([upper, lower], axis=0)


def adjoint(packed):
    return jnp.concatenate([packed[:, :ORB].T, -packed[:, ORB:].T], axis=1)


def cmul(a, b):
    return a[0] * b[0] - a[1] * b[1], a[0] * b[1] + a[1] * b[0]


def cadd(a, b):
    return a[0] + b[0], a[1] + b[1]


def lanes(x, j):
    return jnp.broadcast_to(x[..., j : j + 1], x.shape)


def sublanes(tile, k):
    return jnp.take_along_axis(tile, jnp.full((8, 128), k, jnp.int32), axis=0)


def pivots(real, imag, own, others):
    lane = lax.broadcasted_iota(jnp.int32, (8, 128), 1)
    row = lax.broadcasted_iota(jnp.int32, (8, 128), 0)
    j = 8 * own
    cols = {
        u: [(lanes(real[u], j + c), lanes(imag[u], j + c)) for c in range(8)]
        for u in [own] + others
    }
    ahead = list(cols[own])
    whole = (real[own], imag[own])
    for a in range(8):
        pr, pi = sublanes(ahead[a][0], a), sublanes(ahead[a][1], a)
        scale = 1.0 / (pr * pr + pi * pi)
        is_row = row == a
        factor = (jnp.where(is_row, -1.0, ahead[a][0]), jnp.where(is_row, 0.0, ahead[a][1]))
        factor = cmul(factor, (pr, -pi))

        def eliminate(y, is_col):
            er, ei = sublanes(y[0], a), sublanes(y[1], a)
            br, bi = jnp.where(is_row, 0.0, y[0]), jnp.where(is_row, 0.0, y[1])
            if is_col is not None:
                er, ei = jnp.where(is_col, 1.0, er), jnp.where(is_col, 0.0, ei)
                br, bi = jnp.where(is_col, 0.0, br), jnp.where(is_col, 0.0, bi)
            scaled = cmul(factor, (er, ei))
            return br - scaled[0] * scale, bi - scaled[1] * scale

        for c in range(a + 1, 8):
            ahead[c] = eliminate(ahead[c], None)
        whole = eliminate(whole, lane == j + a)
    real[own], imag[own] = whole
    rows = [(sublanes(whole[0], c), sublanes(whole[1], c)) for c in range(8)]
    inside = (lane >= j) & (lane < j + 8)
    for u in others:
        terms = [cmul(cols[u][c], rows[c]) for c in range(8)]
        while len(terms) > 1:
            terms = [cadd(terms[2 * q], terms[2 * q + 1]) for q in range(len(terms) // 2)]
        real[u] = jnp.where(inside, 0.0, real[u]) - terms[0][0]
        imag[u] = jnp.where(inside, 0.0, imag[u]) - terms[0][1]


def invert(matrix):
    count, extra = ORB // 8, 2
    panel = PANEL // 8
    lane = lax.broadcasted_iota(jnp.int32, (8, 128), 1)
    real = [matrix[8 * u : 8 * u + 8, :ORB] for u in range(count)]
    imag = [matrix[8 * u : 8 * u + 8, ORB:] for u in range(count)]
    for start in range(0, count, panel):
        own = list(range(start, start + panel))
        soon = list(range(start + panel, min(start + panel + extra, count)))
        rest = [u % count for u in range(start + panel, start + count)]
        rest = [u for u in rest if u not in soon]
        s = slice(8 * start, 8 * start + PANEL)
        col_real = {u: real[u][:, s] for u in rest}
        col_imag = {u: imag[u][:, s] for u in rest}
        for q, t in enumerate(own):
            pivots(real, imag, t, own[q + 1 :] + soon + own[:q])
        table = rep(
            jnp.concatenate(
                [
                    jnp.concatenate([real[u] for u in own], axis=0),
                    jnp.concatenate([imag[u] for u in own], axis=0),
                ],
                axis=1,
            )
        )
        inside = (lane >= 8 * start) & (lane < 8 * start + PANEL)
        cut = panel - extra if soon else len(rest)
        for chunk in (rest[:cut], rest[cut:]):
            if chunk:
                sides = [
                    jnp.concatenate([col_real[u] for u in chunk], axis=0),
                    jnp.concatenate([col_imag[u] for u in chunk], axis=0),
                ]
                delta = product(jnp.concatenate(sides, axis=1), table)
                for n, u in enumerate(chunk):
                    part = delta[8 * n : 8 * n + 8]
                    real[u] = jnp.where(inside, 0.0, real[u]) - part[:, :ORB]
                    imag[u] = jnp.where(inside, 0.0, imag[u]) - part[:, ORB:]
    return jnp.concatenate(
        [jnp.concatenate(real, axis=0), jnp.concatenate(imag, axis=0)], axis=1
    )


PACKED = pltpu.VMEM((ORB, 2 * ORB), F32)
DOUBLE = pltpu.VMEM((ORB, 4 * ORB), F32)
VM = pl.BlockSpec(memory_space=pltpu.VMEM)
W = 2 * ORB


def packed(raw):
    return jnp.concatenate([raw[0, 0], raw[0, 1]], axis=1)


def first_kernel(onsite, coupling, diag_out, upper_out, even_out, odd_out):
    position = lax.axis_index("chain")
    energy = -2.0 + 4.0 * lax.axis_index("energy").astype(F32) / lax.axis_size("energy")
    row = lax.broadcasted_iota(jnp.int32, (ORB, ORB), 0)
    column = lax.broadcasted_iota(jnp.int32, (ORB, ORB), 1)
    eye = row == column
    raw_real, raw_imag = onsite[0, 0], onsite[0, 1]
    real = jnp.where(eye, energy, 0.0) - 0.5 * (raw_real + raw_real.T)
    imag = jnp.where(eye, BROADENING, 0.0) - 0.5 * (raw_imag - raw_imag.T)
    diag_out[...] = jnp.concatenate([real, imag], axis=1)
    upper_out[...] = packed(coupling)

    @pl.when(position == CHAINS - 1)
    def contact():
        coupler = packed(coupling)
        square = product(coupler, rep(adjoint(coupler)))
        diag_out[:, :ORB] = real - 0.5 * square[:, ORB:]
        diag_out[:, ORB:] = imag + 0.5 * square[:, :ORB]
        upper_out[...] = jnp.zeros_like(coupler)

    inverse = invert(diag_out[...])
    upper = upper_out[...]
    table = rep(upper)
    onward = product(adjoint(upper), rep(inverse))
    up = jnp.concatenate([product(onward, table), onward], axis=1)
    down = jnp.concatenate([inverse, product(inverse, table)], axis=1)
    even = position % 2 == 0

    @pl.when(even)
    def store_even():
        even_out[...] = up
        odd_out[...] = down

    @pl.when(jnp.logical_not(even))
    def store_odd():
        even_out[...] = down
        odd_out[...] = up


def second_kernel(
    diag, coupler, before, odd_in, even_in, diag_out, lower_out, upper_out, send_out
):
    even = lax.axis_index("chain") % 2 == 0
    left = jnp.where(even, odd_in[...], even_in[...])
    right = jnp.where(even, even_in[...], odd_in[...])
    upper = coupler[...]
    from_right = product(product(upper, rep(right[:, :W])), rep(adjoint(upper)))
    new_diag = diag[...] - left[:, :W] - from_right
    diag_out[...] = new_diag
    new_lower = -product(left[:, W:], rep(adjoint(packed(before))))
    new_upper = -product(upper, rep(right[:, W:]))
    lower_out[...] = new_lower
    upper_out[...] = new_upper
    inverse = invert(new_diag)
    send_out[:, :W] = product(inverse, rep(new_upper))
    send_out[:, W:] = product(inverse, rep(new_lower))


def third_kernel(
    diag, lower, upper, left, right, diag_out, lower_out, upper_out, upward_out, downward_out
):
    sides = jnp.concatenate([lower[...], upper[...]], axis=1)
    tables = jnp.concatenate([rep(left[:, :W]), rep(right[:, W:])], axis=0)
    new_diag = diag[...] - product(sides, tables)
    diag_out[...] = new_diag
    new_lower = -product(lower[...], rep(left[:, W:]))
    new_upper = -product(upper[...], rep(right[:, :W]))
    lower_out[...] = new_lower
    upper_out[...] = new_upper
    inverse = invert(new_diag)
    upward_out[...] = product(inverse, rep(new_upper))
    downward_out[...] = product(inverse, rep(new_lower))


def fourth_kernel(diag, lower, upper, left, right, diag_out, side_out, send_out):
    sides = jnp.concatenate([lower[...], upper[...]], axis=1)
    tables = jnp.concatenate([rep(left[...]), rep(right[...])], axis=0)
    new_diag = diag[...] - product(sides, tables)
    diag_out[...] = new_diag
    side = jnp.where(lax.axis_index("chain") < CHAINS // 2, upper[...], lower[...])
    side_out[...] = side
    send_out[...] = product(invert(new_diag), rep(side))


def last_kernel(diag, side, left, right, left_late, right_late, partner, retained, out):
    low = lax.axis_index("chain") < CHAINS // 2
    outer = product(side[...], rep(left_late[...] + right_late[...]))
    near_side = jnp.where(low, right[...], left[...])
    inner = product(partner[...], rep(near_side))
    green = invert(diag[...] - product(outer, rep(inner)))
    real, imag = green[:, :ORB], green[:, ORB:]
    stack = jnp.concatenate([real.T, imag.T, real, imag], axis=0)
    high = stack.astype(jnp.bfloat16)
    middle = (stack - high.astype(F32)).astype(jnp.bfloat16)
    table = jnp.concatenate([high, middle], axis=1)
    rows = lax.broadcasted_iota(jnp.int32, (ORB, 256), 0)

    def chunk(step, carry):
        index = retained[0:1, pl.ds(pl.multiple_of(step * 256, 256), 256)]
        first = rows == (index >> 7)
        second = rows == (index & 127)
        hot = jnp.where(first, 1.0, 0.0).astype(jnp.bfloat16)
        picked = jnp.dot(
            table, jnp.concatenate([hot, hot], axis=0), preferred_element_type=F32
        )
        tile = []
        for part in range(4):
            chosen = jnp.where(second, picked[part * ORB : (part + 1) * ORB], 0.0)
            partial = jnp.sum(chosen.reshape(16, 8, 256), axis=0)
            for half in range(2):
                piece = partial[:, half * 128 : (half + 1) * 128]
                tile.append(jnp.sum(piece, axis=0, keepdims=True))
        out[step] = jnp.concatenate(tile, axis=0)
        return carry

    lax.fori_loop(0, 32, chunk, 0, unroll=UNROLL)


def correlate_kernel(received, out, second_real, second_imag):
    for half in range(2):
        s = slice(half * 128, (half + 1) * 128)
        ar = received[pl.ds(0 + half, 32, stride=8), :]
        ai = received[pl.ds(2 + half, 32, stride=8), :]
        br = received[pl.ds(4 + half, 32, stride=8), :]
        bi = received[pl.ds(6 + half, 32, stride=8), :]
        second_real[0:32, :] = br
        second_real[32:64, :] = br
        second_imag[0:32, :] = bi
        second_imag[32:64, :] = bi
        total_real = jnp.zeros((32, 128), F32)
        total_imag = jnp.zeros((32, 128), F32)
        for n in range(32):
            x = (
                jnp.broadcast_to(ar[n : n + 1, :], (32, 128)),
                jnp.broadcast_to(ai[n : n + 1, :], (32, 128)),
            )
            term = cmul(x, (second_real[n : n + 32, :], second_imag[n : n + 32, :]))
            total_real += term[0]
            total_imag += term[1]
        out[0, :, 0, s] = total_real
        out[1, :, 0, s] = total_imag


def near(*arrays):
    return [pltpu.with_memory_space_constraint(x, pltpu.VMEM) for x in arrays]


def green_pairs(onsite, coupling, retained):
    def moved(value, by):
        pairs = [(i, i + by) for i in range(CHAINS) if 0 <= i + by < CHAINS]
        return lax.ppermute(value, "chain", pairs)

    def swapped(value, start):
        pairs = [(i, i + 1) for i in range(start, CHAINS - 1, 2)]
        return lax.ppermute(value, "chain", pairs + [(b, a) for a, b in pairs])

    before = moved(coupling, 2)
    diag, upper, even_send, odd_send = pl.pallas_call(
        first_kernel,
        in_specs=[VM, VM],
        out_specs=[VM] * 4,
        out_shape=[PACKED, PACKED, DOUBLE, DOUBLE],
    )(onsite, coupling)
    before, even_send, odd_send = lax.optimization_barrier((before, even_send, odd_send))
    odd_in = swapped(odd_send, 1)
    even_in = swapped(even_send, 0)
    diag, lower, upper, send = pl.pallas_call(
        second_kernel,
        in_specs=[VM] * 5,
        out_specs=[VM] * 4,
        out_shape=[PACKED, PACKED, PACKED, DOUBLE],
    )(*near(diag, upper, before, odd_in, even_in))
    left = moved(send, 2)
    right = moved(send, -2)
    diag, lower, upper, upward, downward = pl.pallas_call(
        third_kernel,
        in_specs=[VM] * 5,
        out_specs=[VM] * 5,
        out_shape=[PACKED] * 5,
    )(*near(diag, lower, upper, left, right))
    left = moved(upward, 4)
    right = moved(downward, -4)
    middle = range(CHAINS // 4, 3 * CHAINS // 4)
    left_late = lax.ppermute(downward, "chain", [(i, i + 4) for i in middle])
    right_late = lax.ppermute(upward, "chain", [(i, i - 4) for i in middle])
    diag, side, send = pl.pallas_call(
        fourth_kernel,
        in_specs=[VM] * 5,
        out_specs=[VM] * 3,
        out_shape=[PACKED] * 3,
    )(*near(diag, lower, upper, left, right))
    send, left_late, right_late = lax.optimization_barrier((send, left_late, right_late))
    partner = lax.ppermute(send, "chain", [(i, (i + 8) % CHAINS) for i in range(CHAINS)])
    return pl.pallas_call(
        last_kernel,
        in_specs=[VM] * 8,
        out_specs=VM,
        out_shape=pltpu.VMEM((32, 8, 128), F32),
    )(*near(diag, side, left, right, left_late, right_late, partner, retained))


def correlate(received):
    return pl.pallas_call(
        correlate_kernel,
        in_specs=[VM],
        out_shape=jax.ShapeDtypeStruct((2, 32, 1, 256), F32),
        scratch_shapes=[pltpu.VMEM((64, 128), F32), pltpu.VMEM((64, 128), F32)],
    )(*near(received.reshape(256, 128)))


def shards(onsite, coupling, retained):
    gathered = green_pairs(onsite, coupling, retained)
    received = lax.all_to_all(gathered, "energy", split_axis=0, concat_axis=0, tiled=True)
    return correlate(received)


def solution(mesh):
    in_specs = (P("chain", None, None, None), P("chain", None, None, None), P("chain", None))
    out_specs = P(None, None, "chain", "energy")
    return jax.shard_map(shards, mesh=mesh, in_specs=in_specs, out_specs=out_specs, check_vma=False)
```

```python
import jax
import jax.numpy as jnp
from jax import lax
from jax.experimental import pallas as pl
from jax.experimental.pallas import tpu as pltpu
from jax.sharding import PartitionSpec as P

ORB = 128
BROADENING = 0.04
PANEL = 32
UNROLL = 16
F32 = jnp.float32
CHAINS = 16


def product(left, right):
    return jnp.dot(left, right, precision=lax.Precision.HIGHEST, preferred_element_type=F32)


def rep(packed):
    real, imag = packed[:, :ORB], packed[:, ORB:]
    upper = jnp.concatenate([real, imag], axis=1)
    lower = jnp.concatenate([-imag, real], axis=1)
    return jnp.concatenate([upper, lower], axis=0)


def adjoint(packed):
    return jnp.concatenate([packed[:, :ORB].T, -packed[:, ORB:].T], axis=1)


def cmul(a, b):
    return a[0] * b[0] - a[1] * b[1], a[0] * b[1] + a[1] * b[0]


def cadd(a, b):
    return a[0] + b[0], a[1] + b[1]


def lanes(x, j):
    return jnp.broadcast_to(x[..., j : j + 1], x.shape)


def sublanes(tile, k):
    return jnp.take_along_axis(tile, jnp.full((8, 128), k, jnp.int32), axis=0)


def pivots(real, imag, own, others):
    lane = lax.broadcasted_iota(jnp.int32, (8, 128), 1)
    row = lax.broadcasted_iota(jnp.int32, (8, 128), 0)
    j = 8 * own
    cols = {
        u: [(lanes(real[u], j + c), lanes(imag[u], j + c)) for c in range(8)]
        for u in [own] + others
    }
    ahead = list(cols[own])
    whole = (real[own], imag[own])
    for a in range(8):
        pr, pi = sublanes(ahead[a][0], a), sublanes(ahead[a][1], a)
        scale = 1.0 / (pr * pr + pi * pi)
        is_row = row == a
        factor = (jnp.where(is_row, -1.0, ahead[a][0]), jnp.where(is_row, 0.0, ahead[a][1]))
        factor = cmul(factor, (pr, -pi))

        def eliminate(y, is_col):
            er, ei = sublanes(y[0], a), sublanes(y[1], a)
            br, bi = jnp.where(is_row, 0.0, y[0]), jnp.where(is_row, 0.0, y[1])
            if is_col is not None:
                er, ei = jnp.where(is_col, 1.0, er), jnp.where(is_col, 0.0, ei)
                br, bi = jnp.where(is_col, 0.0, br), jnp.where(is_col, 0.0, bi)
            scaled = cmul(factor, (er, ei))
            return br - scaled[0] * scale, bi - scaled[1] * scale

        for c in range(a + 1, 8):
            ahead[c] = eliminate(ahead[c], None)
        whole = eliminate(whole, lane == j + a)
    real[own], imag[own] = whole
    rows = [(sublanes(whole[0], c), sublanes(whole[1], c)) for c in range(8)]
    inside = (lane >= j) & (lane < j + 8)
    for u in others:
        terms = [cmul(cols[u][c], rows[c]) for c in range(8)]
        while len(terms) > 1:
            terms = [cadd(terms[2 * q], terms[2 * q + 1]) for q in range(len(terms) // 2)]
        real[u] = jnp.where(inside, 0.0, real[u]) - terms[0][0]
        imag[u] = jnp.where(inside, 0.0, imag[u]) - terms[0][1]


def invert(matrix):
    count, extra = ORB // 8, 2
    panel = PANEL // 8
    lane = lax.broadcasted_iota(jnp.int32, (8, 128), 1)
    real = [matrix[8 * u : 8 * u + 8, :ORB] for u in range(count)]
    imag = [matrix[8 * u : 8 * u + 8, ORB:] for u in range(count)]
    for start in range(0, count, panel):
        own = list(range(start, start + panel))
        soon = list(range(start + panel, min(start + panel + extra, count)))
        rest = [u % count for u in range(start + panel, start + count)]
        rest = [u for u in rest if u not in soon]
        s = slice(8 * start, 8 * start + PANEL)
        col_real = {u: real[u][:, s] for u in rest}
        col_imag = {u: imag[u][:, s] for u in rest}
        for q, t in enumerate(own):
            pivots(real, imag, t, own[q + 1 :] + soon + own[:q])
        table = rep(
            jnp.concatenate(
                [
                    jnp.concatenate([real[u] for u in own], axis=0),
                    jnp.concatenate([imag[u] for u in own], axis=0),
                ],
                axis=1,
            )
        )
        inside = (lane >= 8 * start) & (lane < 8 * start + PANEL)
        cut = panel - extra if soon else len(rest)
        for chunk in (rest[:cut], rest[cut:]):
            if chunk:
                sides = [
                    jnp.concatenate([col_real[u] for u in chunk], axis=0),
                    jnp.concatenate([col_imag[u] for u in chunk], axis=0),
                ]
                delta = product(jnp.concatenate(sides, axis=1), table)
                for n, u in enumerate(chunk):
                    part = delta[8 * n : 8 * n + 8]
                    real[u] = jnp.where(inside, 0.0, real[u]) - part[:, :ORB]
                    imag[u] = jnp.where(inside, 0.0, imag[u]) - part[:, ORB:]
    return jnp.concatenate(
        [jnp.concatenate(real, axis=0), jnp.concatenate(imag, axis=0)], axis=1
    )


PACKED = pltpu.VMEM((ORB, 2 * ORB), F32)
DOUBLE = pltpu.VMEM((ORB, 4 * ORB), F32)
VM = pl.BlockSpec(memory_space=pltpu.VMEM)
W = 2 * ORB


def packed(raw):
    return jnp.concatenate([raw[0, 0], raw[0, 1]], axis=1)


def first_kernel(onsite, coupling, diag_out, upper_out, even_out, odd_out):
    position = lax.axis_index("chain")
    energy = -2.0 + 4.0 * lax.axis_index("energy").astype(F32) / lax.axis_size("energy")
    row = lax.broadcasted_iota(jnp.int32, (ORB, ORB), 0)
    column = lax.broadcasted_iota(jnp.int32, (ORB, ORB), 1)
    eye = row == column
    raw_real, raw_imag = onsite[0, 0], onsite[0, 1]
    real = jnp.where(eye, energy, 0.0) - 0.5 * (raw_real + raw_real.T)
    imag = jnp.where(eye, BROADENING, 0.0) - 0.5 * (raw_imag - raw_imag.T)
    diag_out[...] = jnp.concatenate([real, imag], axis=1)
    upper_out[...] = packed(coupling)

    @pl.when(position == CHAINS - 1)
    def contact():
        coupler = packed(coupling)
        square = product(coupler, rep(adjoint(coupler)))
        diag_out[:, :ORB] = real - 0.5 * square[:, ORB:]
        diag_out[:, ORB:] = imag + 0.5 * square[:, :ORB]
        upper_out[...] = jnp.zeros_like(coupler)

    inverse = invert(diag_out[...])
    upper = upper_out[...]
    table = rep(upper)
    onward = product(adjoint(upper), rep(inverse))
    up = jnp.concatenate([product(onward, table), onward], axis=1)
    down = jnp.concatenate([inverse, product(inverse, table)], axis=1)
    even = position % 2 == 0

    @pl.when(even)
    def store_even():
        even_out[...] = up
        odd_out[...] = down

    @pl.when(jnp.logical_not(even))
    def store_odd():
        even_out[...] = down
        odd_out[...] = up


def second_kernel(
    diag, coupler, before, odd_in, even_in, diag_out, lower_out, upper_out, send_out
):
    even = lax.axis_index("chain") % 2 == 0
    left = jnp.where(even, odd_in[...], even_in[...])
    right = jnp.where(even, even_in[...], odd_in[...])
    upper = coupler[...]
    from_right = product(product(upper, rep(right[:, :W])), rep(adjoint(upper)))
    new_diag = diag[...] - left[:, :W] - from_right
    diag_out[...] = new_diag
    new_lower = -product(left[:, W:], rep(adjoint(packed(before))))
    new_upper = -product(upper, rep(right[:, W:]))
    lower_out[...] = new_lower
    upper_out[...] = new_upper
    inverse = invert(new_diag)
    send_out[:, :W] = product(inverse, rep(new_upper))
    send_out[:, W:] = product(inverse, rep(new_lower))


def third_kernel(
    diag, lower, upper, left, right, diag_out, lower_out, upper_out, upward_out, downward_out
):
    sides = jnp.concatenate([lower[...], upper[...]], axis=1)
    tables = jnp.concatenate([rep(left[:, :W]), rep(right[:, W:])], axis=0)
    new_diag = diag[...] - product(sides, tables)
    diag_out[...] = new_diag
    new_lower = -product(lower[...], rep(left[:, W:]))
    new_upper = -product(upper[...], rep(right[:, :W]))
    lower_out[...] = new_lower
    upper_out[...] = new_upper
    inverse = invert(new_diag)
    upward_out[...] = product(inverse, rep(new_upper))
    downward_out[...] = product(inverse, rep(new_lower))


def fourth_kernel(diag, lower, upper, left, right, diag_out, side_out, send_out):
    sides = jnp.concatenate([lower[...], upper[...]], axis=1)
    tables = jnp.concatenate([rep(left[...]), rep(right[...])], axis=0)
    new_diag = diag[...] - product(sides, tables)
    diag_out[...] = new_diag
    side = jnp.where(lax.axis_index("chain") < CHAINS // 2, upper[...], lower[...])
    side_out[...] = side
    send_out[...] = product(invert(new_diag), rep(side))


def last_kernel(diag, side, left, right, left_late, right_late, partner, retained, hot, out):
    low = lax.axis_index("chain") < CHAINS // 2
    outer = product(side[...], rep(left_late[...] + right_late[...]))
    near_side = jnp.where(low, right[...], left[...])
    inner = product(partner[...], rep(near_side))
    green = invert(diag[...] - product(outer, rep(inner)))
    real, imag = green[:, :ORB], green[:, ORB:]
    stack = jnp.concatenate([real.T, imag.T, real, imag], axis=0)
    high = stack.astype(jnp.bfloat16)
    middle = (stack - high.astype(F32)).astype(jnp.bfloat16)
    table = jnp.concatenate([high, middle], axis=1)
    rows = lax.broadcasted_iota(jnp.int32, (ORB, 256), 0)

    def chunk(step, carry):
        s = pl.ds(pl.multiple_of(step * 256, 256), 256)
        first, second = hot[:, s], rows == (retained[0:1, s] & 127)
        picked = jnp.dot(
            table, jnp.concatenate([first, first], axis=0), preferred_element_type=F32
        )
        tile = []
        for part in range(4):
            chosen = jnp.where(second, picked[part * ORB : (part + 1) * ORB], 0.0)
            partial = jnp.sum(chosen.reshape(16, 8, 256), axis=0)
            for half in range(2):
                piece = partial[:, half * 128 : (half + 1) * 128]
                tile.append(jnp.sum(piece, axis=0, keepdims=True))
        out[step] = jnp.concatenate(tile, axis=0)
        return carry

    lax.fori_loop(0, 32, chunk, 0, unroll=UNROLL)


def hot_kernel(retained, hot):
    rows = lax.broadcasted_iota(jnp.int32, (ORB, 256), 0)

    def chunk(step, carry):
        s = pl.ds(pl.multiple_of(step * 256, 256), 256)
        index = retained[0:1, s]
        hot[:, s] = jnp.where(rows == (index >> 7), 1.0, 0.0).astype(jnp.bfloat16)
        return carry

    lax.fori_loop(0, 32, chunk, 0, unroll=8)


def correlate_kernel(received, out, second_real, second_imag):
    for half in range(2):
        s = slice(half * 128, (half + 1) * 128)
        ar = received[pl.ds(0 + half, 32, stride=8), :]
        ai = received[pl.ds(2 + half, 32, stride=8), :]
        br = received[pl.ds(4 + half, 32, stride=8), :]
        bi = received[pl.ds(6 + half, 32, stride=8), :]
        second_real[0:32, :] = br
        second_real[32:64, :] = br
        second_imag[0:32, :] = bi
        second_imag[32:64, :] = bi
        total_real = jnp.zeros((32, 128), F32)
        total_imag = jnp.zeros((32, 128), F32)
        for n in range(32):
            x = (
                jnp.broadcast_to(ar[n : n + 1, :], (32, 128)),
                jnp.broadcast_to(ai[n : n + 1, :], (32, 128)),
            )
            term = cmul(x, (second_real[n : n + 32, :], second_imag[n : n + 32, :]))
            total_real += term[0]
            total_imag += term[1]
        out[0, :, 0, s] = total_real
        out[1, :, 0, s] = total_imag


def near(*arrays):
    return [pltpu.with_memory_space_constraint(x, pltpu.VMEM) for x in arrays]


def green_pairs(onsite, coupling, retained):
    def moved(value, by):
        pairs = [(i, i + by) for i in range(CHAINS) if 0 <= i + by < CHAINS]
        return lax.ppermute(value, "chain", pairs)

    def swapped(value, start):
        pairs = [(i, i + 1) for i in range(start, CHAINS - 1, 2)]
        return lax.ppermute(value, "chain", pairs + [(b, a) for a, b in pairs])

    before = moved(coupling, 2)
    diag, upper, even_send, odd_send = pl.pallas_call(
        first_kernel,
        in_specs=[VM, VM],
        out_specs=[VM] * 4,
        out_shape=[PACKED, PACKED, DOUBLE, DOUBLE],
    )(onsite, coupling)
    before, even_send, odd_send = lax.optimization_barrier((before, even_send, odd_send))
    odd_in = swapped(odd_send, 1)
    even_in = swapped(even_send, 0)
    diag, lower, upper, send = pl.pallas_call(
        second_kernel,
        in_specs=[VM] * 5,
        out_specs=[VM] * 4,
        out_shape=[PACKED, PACKED, PACKED, DOUBLE],
    )(*near(diag, upper, before, odd_in, even_in))
    left = moved(send, 2)
    right = moved(send, -2)
    diag, lower, upper, upward, downward = pl.pallas_call(
        third_kernel,
        in_specs=[VM] * 5,
        out_specs=[VM] * 5,
        out_shape=[PACKED] * 5,
    )(*near(diag, lower, upper, left, right))
    left = moved(upward, 4)
    right = moved(downward, -4)
    middle = range(CHAINS // 4, 3 * CHAINS // 4)
    left_late = lax.ppermute(downward, "chain", [(i, i + 4) for i in middle])
    right_late = lax.ppermute(upward, "chain", [(i, i - 4) for i in middle])
    diag, side, send = pl.pallas_call(
        fourth_kernel,
        in_specs=[VM] * 5,
        out_specs=[VM] * 3,
        out_shape=[PACKED] * 3,
    )(*near(diag, lower, upper, left, right))
    send, left_late, right_late, listed = lax.optimization_barrier(
        (send, left_late, right_late, retained)
    )
    partner = lax.ppermute(send, "chain", [(i, (i + 8) % CHAINS) for i in range(CHAINS)])
    hot = pl.pallas_call(
        hot_kernel,
        in_specs=[VM],
        out_specs=VM,
        out_shape=pltpu.VMEM((ORB, 8192), jnp.bfloat16),
    )(listed)
    return pl.pallas_call(
        last_kernel,
        in_specs=[VM] * 9,
        out_specs=VM,
        out_shape=pltpu.VMEM((32, 8, 128), F32),
    )(*near(diag, side, left, right, left_late, right_late, partner, retained, hot))


def correlate(received):
    return pl.pallas_call(
        correlate_kernel,
        in_specs=[VM],
        out_shape=jax.ShapeDtypeStruct((2, 32, 1, 256), F32),
        scratch_shapes=[pltpu.VMEM((64, 128), F32), pltpu.VMEM((64, 128), F32)],
    )(*near(received.reshape(256, 128)))


def shards(onsite, coupling, retained):
    gathered = green_pairs(onsite, coupling, retained)
    received = lax.all_to_all(gathered, "energy", split_axis=0, concat_axis=0, tiled=True)
    return correlate(received)


def solution(mesh):
    in_specs = (P("chain", None, None, None), P("chain", None, None, None), P("chain", None))
    out_specs = P(None, None, "chain", "energy")
    return jax.shard_map(shards, mesh=mesh, in_specs=in_specs, out_specs=out_specs, check_vma=False)
```
